32 devices in a mesh: in: 4 (over z), out: 8 (over y, x, core).
Axes of the slice: x: 2, y: 2, z: 4, core: 2. Of those that a mesh axis runs over, the one named last changes fastest.
Arguments:
- activations: bfloat16 [512, 5120], P('out', 'in'), may hold values from -6 to 6
- act_basis: bfloat16 [5120, 5120], P(None, 'in'), may hold values from -0.078125 to 0.078125
- gradients: bfloat16 [512, 20480], P('out', 'in'), may hold values from -0.59765625 to 0.59765625
- grad_basis: bfloat16 [20480, 20480], P('in', 'out'), may hold values from -0.0390625 to 0.0390625
- lengths: int32 [4], replicated, may hold values from 1 to 128, 384 in all
- sample_weights: int32 [4], replicated, may hold values from 1 to 4
Outputs:
- eigenvalues: float32 [20480, 5120], P('out', 'in')
The draws below stay inside these ranges and needn't reach their ends.
Inputs may be any that keep to these rules, and one draw needn't show every extreme that they name: Some sequence is full, every sequence has at least one valid token, and the lengths sum to 384.
All inputs are finite; a program needn't handle non-finite values.
Results may differ from the reference program's by a relative error of at most 0.0031.
Values may be sent and summed in bfloat16 or wider, within the bound.
No kernel may reach another device: no remote copies, remote signals or barrier semaphores. Data moves between devices by JAX's collectives and lax.ppermute only.
A program may use at most 128 MiB of HBM per device.

```python
import math
import jax
import jax.numpy as jnp
import numpy as np
from jax import lax

DIN = 5120
DOUT = 20480
LEN = 128
SEQS = 4
TOKENS = 512


def set_ends(array, rng, least, largest):
    spot = [jax.random.randint(jax.random.fold_in(rng, axis), (), 0, length) for axis, length in enumerate(array.shape)]
    main_axis = array.shape.index(max(array.shape))
    next_to = spot[:main_axis] + [(spot[main_axis] + 1) % array.shape[main_axis]] + spot[main_axis + 1:]
    return array.at[tuple(spot)].set(least).at[tuple(next_to)].set(largest)


def levels(own_key, dims, shards, low, largest):
    loudness, own = 1.0, jax.random.fold_in(own_key, 6)
    for axis_at, blocks in shards:
        steps = jnp.exp(jax.random.uniform(jax.random.fold_in(own, axis_at), (blocks,), jnp.float32, low / len(shards), largest / len(shards)))
        loudness = loudness * jnp.repeat(steps, dims[axis_at] // blocks).reshape([-1 if axis == axis_at else 1 for axis in range(len(dims))])
    return loudness


def length_profile(amount, total, bound, slope):
    loads = [(1 << 20) // math.isqrt(rank ** slope) + 1 for rank in range(2, amount + 1)]
    rest, holding = total - bound - (amount - 1), [1] * (amount - 1)
    while rest > 0:
        free = [i for i in range(amount - 1) if holding[i] < bound]
        pool, remaining = sum([loads[i] for i in free]), rest
        for i in free:
            more = min(bound - holding[i], max(1, remaining * loads[i] // pool), rest)
            holding[i] = holding[i] + more
            rest = rest - more
    return np.array([bound] + holding)


def ragged(key, number_of, total, limit, slope):
    if number_of == 2:
        one = jax.random.randint(key, (), max(1, total - limit), min(limit, total - 1) + 1)
        return jnp.stack([one, total - one])
    tallies = jnp.asarray(length_profile(number_of, total, limit, slope), jnp.int32)
    pairs = (number_of - 1) // 2
    giver, sink = tallies[1:1 + 2 * pairs:2], tallies[2:2 + 2 * pairs:2]
    margin = jnp.minimum(giver - 1, limit - sink)
    moved = jax.random.randint(jax.random.fold_in(key, 1), (pairs,), 0, 1 << 20) % (margin + 1)
    tallies = tallies.at[1:1 + 2 * pairs:2].set(giver - moved).at[2:2 + 2 * pairs:2].set(sink + moved)
    return tallies[jax.random.permutation(jax.random.fold_in(key, 2), number_of)]


def bell_draw(rng, shape, width, limit, split=(), kind=jnp.bfloat16):
    result = jax.random.normal(rng, shape, jnp.float32) * width
    if len(split) > 0:
        result = levels(rng, shape, split, -0.22, 0.18) * result
    return jnp.clip(result, min=-limit, max=limit).astype(kind)


def setup_inputs(seed: int = 0) -> dict:
    key_of = jax.random.split(jax.random.key(seed), 7)
    activations = bell_draw(key_of[0], (TOKENS, DIN), 1.0, 6.0, ((0, 8), (1, 4)))
    act_basis = bell_draw(key_of[1], (DIN, DIN), DIN ** -0.5, 0.078125, ((1, 4),))
    gradients = bell_draw(key_of[2], (TOKENS, DOUT), 0.09, 0.59765625, ((0, 8), (1, 4)))
    grad_basis = bell_draw(key_of[3], (DOUT, DOUT), DOUT ** -0.5, 0.0390625, ((0, 4), (1, 8)))
    lengths = ragged(key_of[4], SEQS, SEQS * LEN * 3 // 4, LEN, 2).astype(jnp.int32)
    sample_weights = set_ends(jax.random.randint(key_of[5], (SEQS,), 1, 5), jax.random.fold_in(key_of[5], 1), 1, 4).astype(jnp.int32)
    return {"activations": activations, "act_basis": act_basis, "gradients": gradients, "grad_basis": grad_basis, "lengths": lengths, "sample_weights": sample_weights}


def reference(activations, act_basis, gradients, grad_basis, lengths, sample_weights):
    rot_act = jnp.dot(activations, act_basis, preferred_element_type=jnp.float32).astype(jnp.bfloat16)
    rot_grad = jnp.dot(gradients, grad_basis, preferred_element_type=jnp.float32).astype(jnp.bfloat16)
    positions = jnp.arange(LEN, dtype=jnp.int32)
    valid = (positions[None, :] < lengths[:, None]).astype(rot_grad.dtype)
    act_seq = rot_act.reshape(SEQS, LEN, DIN)
    grad_seq = rot_grad.reshape(SEQS, LEN, DOUT) * valid[:, :, None]
    weights = sample_weights.astype(jnp.float32)

    def accumulate(total, item):
        grad_one, act_one, weight = item
        block = lax.dot_general(grad_one, act_one, (((0,), (0,)), ((), ())), preferred_element_type=jnp.float32)
        return total + weight * block * block, None

    start = jnp.zeros((DOUT, DIN), jnp.float32)
    total, unused = lax.scan(accumulate, start, (grad_seq, act_seq, weights))
    return total / jnp.sum(weights)
```

```python
import jax
import jax.numpy as jnp
from jax import lax
from jax.experimental import pallas as pl
from jax.experimental.pallas import tpu as pltpu
from jax.sharding import PartitionSpec as P

CHUNKS = 2
GROUPS = 5
LAG = 2


def generic(activations, act_basis, gradients, grad_basis, lengths, sample_weights):
    width_in = act_basis.shape[1]
    local_rot = jnp.dot(
        lax.all_gather(activations, "in", axis=1, tiled=True), act_basis, preferred_element_type=jnp.float32
    ).astype(jnp.bfloat16)
    rot_act = lax.all_gather(local_rot, "out", axis=0, tiled=True)
    seq_count = lengths.shape[0]
    slot_count = rot_act.shape[0] // seq_count
    positions = jnp.arange(slot_count, dtype=jnp.int32)
    valid = (positions[None, :] < lengths[:, None]).astype(jnp.bfloat16)
    partial_rot = jnp.dot(
        lax.all_gather(gradients, "out", axis=0, tiled=True), grad_basis, preferred_element_type=jnp.float32
    )
    rot_rows = lax.psum(partial_rot, "in").astype(jnp.bfloat16)
    act_seq = rot_act.reshape(seq_count, slot_count, width_in)
    grad_seq = rot_rows.reshape(seq_count, slot_count, rot_rows.shape[1]) * valid[:, :, None]
    weights = sample_weights.astype(jnp.float32)

    def accumulate(total, item):
        grad_one, act_one, weight = item
        block = lax.dot_general(
            grad_one, act_one, (((0,), (0,)), ((), ())), preferred_element_type=jnp.float32
        )
        return (total + weight * block * block, None)

    start_total = jnp.zeros((rot_rows.shape[1], width_in), jnp.float32)
    total, unused = lax.scan(accumulate, start_total, (grad_seq, act_seq, weights))
    return total / jnp.sum(weights)


def squares_kernel(place_ref, weight_ref, pick_ref, s_ref, even_ref, odd_ref, out_ref):
    count = weight_ref.shape[0]
    half = even_ref.shape[0] // count
    chip = place_ref[0] // 2
    weights = [weight_ref[n].astype(jnp.float32) for n in range(count)]
    whole = weights[0]
    for n in range(1, count):
        whole = whole + weights[n]
    s = jnp.concatenate([ref[...] for ref in s_ref], axis=0)
    total = None
    for n in range(count):
        pick = pick_ref[2 * half * n:2 * half * (n + 1), :]
        rows = jnp.dot(pick, s, preferred_element_type=jnp.float32).astype(jnp.bfloat16)
        acts = jnp.concatenate(
            [even_ref[half * n:half * (n + 1), :], odd_ref[half * n:half * (n + 1), :]], axis=0
        )
        example = lax.dot_general(rows, acts, (((0,), (0,)), ((), ())), preferred_element_type=jnp.float32)
        scale = weight_ref[lax.bitwise_xor(chip, n)].astype(jnp.float32) / whole
        term = (scale * example) * example
        total = term if total is None else total + term
    out_ref[...] = total


def squares(place, sample_weights, pick, parts, even, odd, out, group, height):
    cols = parts[0].shape[1]
    width = even.shape[1]

    def body(place_ref, weight_ref, pick_ref, *rest):
        s_refs, rest = rest[:len(parts)], rest[len(parts):]
        squares_kernel(place_ref, weight_ref, pick_ref, s_refs, rest[0], rest[1], rest[-1])

    tail, aliases = [], {}
    specs = [
        pl.BlockSpec(memory_space=pltpu.SMEM),
        pl.BlockSpec(memory_space=pltpu.SMEM),
        pl.BlockSpec(pick.shape, lambda i: (0, 0)),
    ]
    specs += [pl.BlockSpec(part.shape, lambda i: (0, 0)) for part in parts]
    specs += [pl.BlockSpec(even.shape, lambda i: (0, 0)), pl.BlockSpec(odd.shape, lambda i: (0, 0))]
    if out is not None:
        tail = [out]
        aliases = {len(specs): 0}
        specs.append(pl.BlockSpec(memory_space=pl.ANY))
    return pl.pallas_call(
        body,
        grid=(1,),
        in_specs=specs,
        out_specs=pl.BlockSpec((cols, width), lambda i: (group, 0)),
        out_shape=jax.ShapeDtypeStruct((height, width), jnp.float32),
        input_output_aliases=aliases,
        compiler_params=pltpu.CompilerParams(vmem_limit_bytes=26 << 20),
        cost_estimate=pl.CostEstimate(
            flops=4 * cols * width * pick.shape[0], bytes_accessed=4 * cols * width + 4 * even.size, transcendentals=0
        ),
    )(place, sample_weights, pick, *parts, even, odd, *tail)


def line(activations, act_basis, gradients, grad_basis, lengths, sample_weights):
    bf16, f16 = jnp.bfloat16, jnp.float16
    slots, wide = gradients.shape
    seqs = lengths.shape[0]
    z = lax.axis_index("in")
    o = lax.axis_index("out")

    def swap(x, bit):
        return lax.ppermute(x, "out", [(i, i ^ bit) for i in range(2 * seqs)])

    step = slots // CHUNKS
    mid = wide // 2
    chunks = []
    for k in range(CHUNKS):
        rows = gradients[k * step:(k + 1) * step]
        parts = []
        for cols, bits in ((rows[:, :mid], (2, 4)), (rows[:, mid:], (4, 2))):
            for bit in bits:
                cols = jnp.concatenate([cols, swap(cols, bit)], axis=0)
            parts.append((cols, swap(cols, 1)))
        chunks.append(parts)

    shifted = [activations] + [
        lax.ppermute(activations, "in", [(i, (i + d) % 4) for i in range(4)]) for d in (1, 2, 3)
    ]
    block = activations.shape[1]

    n_of = jnp.arange(seqs, dtype=jnp.int32)
    q_at = jnp.arange(CHUNKS, dtype=jnp.int32)[:, None, None]
    b_at = jnp.arange(2, dtype=jnp.int32)[None, None, :]
    counts = jnp.clip(lengths[None, :, None] - b_at * slots - q_at * step, 0, step)
    counts = counts.reshape(-1)
    label = jnp.arange(counts.shape[0], dtype=jnp.int32)

    def packed_index(q, dev, r):
        mine = (q * seqs + dev // 2) * 2 + dev % 2
        before = jnp.sum(jnp.where(label[None, :] < mine[:, None], counts[None, :], 0), axis=1)
        have = jnp.sum(jnp.where(label[None, :] == mine[:, None], counts[None, :], 0), axis=1)
        return jnp.where(r < have, before + r, -1)

    total_rows = slots * 2 * seqs * 3 // 4
    packed_rows = total_rows // CHUNKS

    def slot_index(order):
        out = []
        pos = jnp.arange(len(order) * step, dtype=jnp.int32)
        dev = lax.bitwise_xor(o, sum(jnp.where(pos // step == i, p, 0) for i, p in enumerate(order)).astype(jnp.int32))
        for q in range(CHUNKS):
            out.append(packed_index(jnp.int32(q), dev, pos % step))
        return out

    first = ((0, 2, 4, 6), (1, 3, 5, 7))
    second = ((0, 4, 2, 6), (1, 5, 3, 7))

    def one_hot(index, start):
        return (index[None, :] == start + jnp.arange(packed_rows, dtype=jnp.int32)[:, None]).astype(bf16)

    packed = []
    for k in range(CHUNKS):
        halves = []
        for side, orders in enumerate((first, second)):
            hots, rows = [], []
            for half in (0, 1):
                index = slot_index(orders[half])
                for q in range(k + 1):
                    hots.append(one_hot(index[q], k * packed_rows))
                    rows.append(chunks[q][side][half])
            halves.append(
                jnp.dot(
                    jnp.concatenate(hots, axis=1), jnp.concatenate(rows, axis=0), preferred_element_type=jnp.float32
                ).astype(bf16)
            )
        packed.append(jnp.concatenate(halves, axis=1))

    height = grad_basis.shape[1]
    cut = height // GROUPS
    tiles = CHUNKS * GROUPS
    own = []
    for k in range(CHUNKS):
        for g in range(GROUPS):
            own.append(
                jnp.dot(
                    packed[k], grad_basis[:, g * cut:(g + 1) * cut], preferred_element_type=jnp.float32
                ).astype(f16)
            )

    outer = (z == 0) | (z == 3)
    inward, outward, middle = [(0, 1), (3, 2)], [(1, 0), (2, 3)], [(1, 2), (2, 1)]
    ends, mids = {}, {}
    for s in range(tiles + 2 * LAG):
        back = s - 2 * LAG
        if back < 0:
            operand, pairs = own[s], inward
        else:
            operand, pairs = own[back] + mids[back], outward
            if s < tiles:
                operand, pairs = jnp.where(outer, own[s], operand), inward + outward
        ends[s] = lax.ppermute(operand, "in", pairs)
        c = s - LAG
        if 0 <= c < tiles:
            mids[c] = lax.ppermute(own[c] + ends[c], "in", middle)
    f32 = jnp.float32
    sums = [
        (
            own[c].astype(f32)
            + jnp.where(outer, ends[c + 2 * LAG], ends[c]).astype(f32)
            + mids[c].astype(f32)
        ).astype(bf16)
        for c in range(tiles)
    ]

    acts = jnp.zeros((activations.shape[0], act_basis.shape[0]), bf16)
    for d, piece in enumerate(shifted):
        acts = lax.dynamic_update_slice(acts, piece, (0, lax.rem(z + 4 - d, 4) * block))
    rot = jnp.dot(acts, act_basis, preferred_element_type=f32).astype(bf16)
    even = jnp.concatenate([rot, swap(rot, 2)], axis=0)
    even = jnp.concatenate([even, swap(even, 4)], axis=0)
    odd = swap(even, 1)

    pos = jnp.arange(2 * seqs * slots, dtype=jnp.int32)
    at = pos // slots
    row = pos % slots
    index = packed_index(row // step, lax.bitwise_xor(o, at), row % step)
    pick = (index[:, None] == jnp.arange(total_rows, dtype=jnp.int32)[None, :]).astype(bf16)

    place = o.reshape(1)
    out = None
    for g in range(GROUPS):
        parts = [sums[k * GROUPS + g] for k in range(CHUNKS)]
        out = squares(place, sample_weights, pick, parts, even, odd, out, g, height)
    return out


def solution(mesh):
    in_specs = (P("out", "in"), P(None, "in"), P("out", "in"), P("in", "out"), P(), P())
    out_specs = P("out", "in")
    body = line if mesh.shape["in"] == 4 and mesh.shape["out"] == 8 else generic
    return jax.shard_map(body, mesh=mesh, in_specs=in_specs, out_specs=out_specs, check_vma=False)
```
